256 devices in a mesh: freq: 16 (over y, x), tile: 16 (over z, core).
Axes of the slice: x: 4, y: 4, z: 8, core: 2. Of those that a mesh axis runs over, the one named last changes fastest.
Arguments:
- x_field: bfloat16 [16, 2, 10240, 256], P('freq', None, 'tile'), may hold values from -6 to 6
- data: bfloat16 [16, 2, 10240, 256], P('freq', None, 'tile'), may hold values from -6 to 6
- u_bases: bfloat16 [16, 16, 16, 128, 2, 640], P('freq', 'tile'), may hold values from -0.15625 to 0.15625
- v_bases: bfloat16 [16, 16, 16, 128, 2, 640], P('freq', None, 'tile'), may hold values from -0.15625 to 0.15625
- ranks: int32 [16, 16, 16], P('freq'), may hold values from 49 to 96, as said below
- onset: int32 [10240, 256], P(('tile', 'freq')), may hold values from 0 to 15
Outputs:
- gradient: float32 [32, 10240, 256], P(None, ('tile', 'freq'))
The draws below stay inside these ranges and needn't reach their ends.
Inputs may be any that keep to these rules, and one draw needn't show every extreme that they name: ranks[f,r,c] is the rank of tile (r, c) at frequency f; it is at most 96, and equal to 96 for some tile of every frequency.
All inputs are finite; a program needn't handle non-finite values.
Results may differ from the reference program's by a relative error of at most 0.0055.
Values may be sent and summed in bfloat16 or wider, within the bound.
A program may use at most 64 MiB of HBM per device.

```python
import math
import jax
import jax.numpy as jnp
from jax import lax

TILE = 640
RPAD = 128
RMAX = 96
RMIN = 49
NVIRT = 256
NTILE = 16
NS = 10240
NF = 16
NT = 32


def draw_ranks(key, part):
    first_key, second_key = jax.random.split(jax.random.fold_in(key, 17))
    sampled = jax.random.randint(first_key, (NF, NTILE * NTILE), RMIN, RMAX + 1)
    chosen = jax.random.randint(second_key, (NF, 1), 0, NTILE * NTILE)
    tile_slots = jnp.arange(NTILE * NTILE, dtype=jnp.int32)[None, :]
    return jnp.where(tile_slots == chosen, RMAX, sampled).reshape(NF, NTILE, NTILE).astype(jnp.int32)


def set_ends(array, own_key, least, top_value):
    longest = array.shape.index(max(array.shape))
    spots = []
    for shift in (0, 1):
        where = [jax.random.randint(jax.random.fold_in(own_key, axis), (), 0, length) for axis, length in enumerate(array.shape)]
        where[longest] = (where[longest] + shift) % array.shape[longest]
        spots.append(tuple(where))
    return array.at[spots[0]].set(least).at[spots[1]].set(top_value)


def level_of(own_key, dims, cuts, least, top_value):
    def one(axis_at, shards_of):
        heights = jax.random.uniform(jax.random.fold_in(jax.random.fold_in(own_key, 6), axis_at), (shards_of,), jnp.float32, least / len(cuts), top_value / len(cuts))
        return jnp.repeat(jnp.exp(heights), dims[axis_at] // shards_of).reshape((-1,) + (1,) * (len(dims) - axis_at - 1))

    level = one(*cuts[0])
    for cut in cuts[1:]:
        level = level * one(*cut)
    return level


def centred(own_key, shape, width, bound, cuts=(), kind=jnp.bfloat16):
    factor_of = level_of(own_key, shape, cuts, -0.22, 0.18) if cuts else 1.0
    result = jax.random.normal(own_key, shape, jnp.float32) * width * factor_of
    return jnp.minimum(jnp.maximum(result, -bound), bound).astype(kind)


def setup_inputs(seed: int = 0) -> dict:
    keys = jax.random.split(jax.random.key(seed), 7)
    return {
        "x_field": centred(keys[0], (NF, 2, NS, NVIRT), 1.0, 6.0, ((0, 16), (2, 16))),
        "data": centred(keys[1], (NF, 2, NS, NVIRT), 1.0, 6.0, ((0, 16), (2, 16))),
        "u_bases": centred(keys[2], (NF, NTILE, NTILE, RPAD, 2, TILE), (NTILE * RMAX) ** -0.5, 0.15625, ((0, 16), (1, 16))),
        "v_bases": centred(keys[3], (NF, NTILE, NTILE, RPAD, 2, TILE), (2 * TILE) ** -0.5, 0.15625, ((0, 16), (2, 16))),
        "ranks": draw_ranks(jax.random.fold_in(keys[6], 71), 0),
        "onset": set_ends(jax.random.randint(keys[5], (NS, NVIRT), 0, NT // 2), jax.random.fold_in(keys[5], 1), 0, (NT // 2) - 1).astype(jnp.int32),
    }


PRECISE = lax.Precision.HIGHEST

def conj_apply(factors, vectors):
    partner = jnp.stack([vectors[1], -vectors[0]])
    stacked = jnp.stack([vectors, partner], axis=2)
    return jnp.einsum('nkps,psov->nkov', factors.astype(jnp.float32), stacked.astype(jnp.float32), precision=PRECISE)

def apply_factors(factors, weights):
    real_part = weights[:, :, 0]
    imag_part = weights[:, :, 1]
    blended = jnp.stack([jnp.stack([real_part, imag_part], axis=2), jnp.stack([-imag_part, real_part], axis=2)], axis=2)
    return jnp.einsum('nkps,nkpov->osv', factors.astype(jnp.float32), blended.astype(jnp.float32), precision=PRECISE)

def column_step(operands):
    return conj_apply(operands[0], operands[1])

def row_step(operands):
    return apply_factors(operands[0], operands[1])

def one_frequency(operands):
    u_freq, v_freq, x_freq, d_freq, rank_freq = operands
    rank_mask = (jnp.arange(RPAD, dtype=jnp.int32)[None, None, :] < rank_freq[:, :, None]).astype(jnp.float32)
    x_blocks = jnp.transpose(x_freq.reshape(2, NTILE, TILE, NVIRT), (1, 0, 2, 3))
    d_blocks = jnp.transpose(d_freq.reshape(2, NTILE, TILE, NVIRT), (1, 0, 2, 3))
    v_columns = jnp.moveaxis(v_freq, 1, 0)
    coeffs = jnp.moveaxis(lax.map(column_step, (v_columns, x_blocks)), 0, 1)
    coeffs = (coeffs * rank_mask[:, :, :, None, None]).astype(jnp.bfloat16)
    predicted = lax.map(row_step, (u_freq, coeffs))
    residual = (predicted - d_blocks.astype(jnp.float32)).astype(jnp.bfloat16)
    adjoint = lax.map(column_step, (u_freq, residual))
    adjoint = (adjoint * rank_mask[:, :, :, None, None]).astype(jnp.bfloat16)
    spectra = lax.map(row_step, (v_columns, jnp.moveaxis(adjoint, 0, 1)))
    return spectra.astype(jnp.bfloat16)

def reference(x_field, data, u_bases, v_bases, ranks, onset):
    spectra = lax.map(one_frequency, (u_bases, v_bases, x_field, data, ranks))
    spectra = jnp.transpose(spectra, (0, 2, 1, 3, 4)).reshape(NF, 2, NS, NVIRT).astype(jnp.float32)
    moments = jnp.arange(NT, dtype=jnp.int32)
    orders = jnp.arange(1, NF + 1, dtype=jnp.int32)
    phases = moments[:, None] * orders[None, :] % NT
    angles = 2.0 * math.pi / NT * phases.astype(jnp.float32)
    cosine = jnp.cos(angles)
    sine_part = jnp.sin(angles)
    traces = jnp.dot(cosine, spectra[:, 0].reshape(NF, -1), precision=PRECISE) - jnp.dot(sine_part, spectra[:, 1].reshape(NF, -1), precision=PRECISE)
    traces = (traces * (1.0 / math.sqrt(NF))).reshape(NT, NS, NVIRT)
    return jnp.where(moments[:, None, None] >= onset[None], traces, jnp.float32(0.0))
```

```python
import functools
import math

import jax
import jax.numpy as jnp
from jax import lax
from jax.experimental import pallas as pl
from jax.experimental.pallas import tpu as pltpu
from jax.sharding import PartitionSpec as P

RMAX = 96
HALF = 128
MESH = pl.DeviceIdType.MESH
CONTRACT_ROWS = (((0,), (0,)), ((), ()))


def hop(slot):
    step = slot // 2
    quarter = step // 2
    odd = step % 2
    return 4 + quarter - odd * (2 * quarter + 1), (slot + slot // 14) % 2


def tile_at(position, slot, sign):
    chips, cores = hop(slot)
    return (position // 2 + sign * chips + 8) % 8 * 2 + (position % 2 + cores) % 2


def freq_at(position, slot):
    return (position // 4 + slot // 4) % 4 * 4 + (position % 4 + slot % 4) % 4


def exchange_kernel(
    ranks_ref, x_hbm, d_hbm, u_hbm, v_hbm, out_ref,
    x_mat, x_rot, d_mat, v_raw, u_raw, v_mat, u_mat, total,
    c_send, c_recv, a_send, a_recv, f_send, f_recv,
    load_sem, v_sem, u_sem, c_sems, a_sems, f_sems, out_sem,
):
    freq = lax.axis_index("freq")
    tile = lax.axis_index("tile")
    barrier = pltpu.get_barrier_semaphore()

    def greet_tile(slot, carry):
        pl.semaphore_signal(barrier, inc=1, device_id=(freq, tile_at(tile, slot, 1)), device_id_type=MESH)
        return carry

    def greet_freq(slot, carry):
        pl.semaphore_signal(barrier, inc=1, device_id=(freq_at(freq, slot), tile), device_id_type=MESH)
        return carry

    lax.fori_loop(0, 15, greet_tile, 0)
    lax.fori_loop(1, 16, greet_freq, 0)

    def field_copy(source, target, half, part, index):
        return pltpu.make_async_copy(
            source.at[0, part, :, pl.ds(half * HALF, HALF)],
            target.at[half, :, pl.ds(part * HALF, HALF)],
            load_sem.at[index, half, part],
        )

    def v_copy(slot):
        return pltpu.make_async_copy(
            v_hbm.at[0, tile_at(tile, slot, 1), 0, pl.ds(0, RMAX)], v_raw.at[slot], v_sem.at[slot]
        )

    def u_copy(slot):
        return pltpu.make_async_copy(
            u_hbm.at[0, 0, tile_at(tile, slot, -1), pl.ds(0, RMAX)], u_raw.at[slot], u_sem.at[slot]
        )

    def start_v(slot, carry):
        v_copy(slot).start()
        return carry

    def start_u(slot, carry):
        u_copy(slot).start()
        return carry

    field_copy(x_hbm, x_mat, 0, 0, 0).start()
    field_copy(x_hbm, x_mat, 0, 1, 0).start()
    lax.fori_loop(0, 16, start_v, 0)
    field_copy(x_hbm, x_mat, 1, 0, 0).start()
    field_copy(x_hbm, x_mat, 1, 1, 0).start()
    lax.fori_loop(0, 16, start_u, 0)
    for half in range(2):
        for part in range(2):
            field_copy(d_hbm, d_mat, half, part, 1).start()

    rows = lax.broadcasted_iota(jnp.int32, (2 * RMAX, 2 * RMAX), 0)
    columns = lax.broadcasted_iota(jnp.int32, (2 * RMAX, 2 * RMAX), 1)
    wanted = jnp.where(rows < RMAX, 2 * rows, 2 * (rows - RMAX) + 1)
    separate = jnp.where(columns == wanted, 1.0, 0.0).astype(jnp.bfloat16)
    levels = lax.broadcasted_iota(jnp.int32, (RMAX, 2 * HALF), 0)

    def separated(raw):
        interleaved = raw.reshape(2 * RMAX, raw.shape[-1])
        return jnp.dot(separate, interleaved, preferred_element_type=jnp.float32).astype(jnp.bfloat16)

    def rotated(field):
        return jnp.concatenate([field[:, HALF:], -field[:, :HALF]], axis=1)

    def conj_apply(basis, slot, field, partner, rank):
        value = jnp.dot(basis[slot, pl.ds(0, RMAX)], field, preferred_element_type=jnp.float32)
        value += jnp.dot(basis[slot, pl.ds(RMAX, RMAX)], partner, preferred_element_type=jnp.float32)
        return jnp.where(levels < rank, value, 0.0).astype(jnp.bfloat16)

    def apply_basis(basis, slot, weights):
        partner = jnp.concatenate([-weights[:, HALF:], weights[:, :HALF]], axis=1)
        blended = jnp.concatenate([weights, partner], axis=0)
        return lax.dot_general(basis[slot], blended, CONTRACT_ROWS, preferred_element_type=jnp.float32)

    def c_copy(half, slot):
        return pltpu.make_async_remote_copy(
            src_ref=c_send.at[half, slot], dst_ref=c_recv.at[half, slot],
            send_sem=c_sems.at[0, half, slot], recv_sem=c_sems.at[1, half, slot],
            device_id=(freq, tile_at(tile, slot, 1)), device_id_type=MESH,
        )

    def a_copy(half, slot):
        return pltpu.make_async_remote_copy(
            src_ref=a_send.at[half, slot], dst_ref=a_recv.at[half, slot],
            send_sem=a_sems.at[0, half, slot], recv_sem=a_sems.at[1, half, slot],
            device_id=(freq, tile_at(tile, slot, -1)), device_id_type=MESH,
        )

    def f_copy(half, slot):
        peer = freq_at(freq, slot)
        return pltpu.make_async_remote_copy(
            src_ref=f_send.at[half, peer], dst_ref=f_recv.at[half, freq],
            send_sem=f_sems.at[0, half, slot], recv_sem=f_sems.at[1, half, slot],
            device_id=(peer, tile), device_id_type=MESH,
        )

    def coefficients(half, slot):
        rank = ranks_ref[0, tile_at(tile, slot, 1), tile]
        return conj_apply(v_mat, slot, x_mat[half], x_rot[half], rank)

    def prepare_v(slot):
        v_copy(slot).wait()
        v_mat[slot] = separated(v_raw[slot])

    def wait_field(half, index, source, target):
        for part in range(2):
            field_copy(source, target, half, part, index).wait()

    wait_field(0, 0, x_hbm, x_mat)
    x_rot[0] = rotated(x_mat[0])
    prepare_v(0)
    c_send[0, 0] = coefficients(0, 0)
    pl.semaphore_wait(barrier, 30)
    c_copy(0, 0).start()

    def send_first(slot, carry):
        prepare_v(slot)
        c_send[0, slot] = coefficients(0, slot)
        c_copy(0, slot).start()
        return carry

    lax.fori_loop(1, 15, send_first, 0)
    prepare_v(15)
    c_recv[0, 15] = coefficients(0, 15)

    wait_field(1, 0, x_hbm, x_mat)
    x_rot[1] = rotated(x_mat[1])

    def send_second(slot, carry):
        c_send[1, slot] = coefficients(1, slot)
        c_copy(1, slot).start()
        return carry

    lax.fori_loop(0, 15, send_second, 0)
    c_recv[1, 15] = coefficients(1, 15)

    def prepare_u(slot, carry):
        u_copy(slot).wait()
        u_mat[slot] = separated(u_raw[slot])
        return carry

    lax.fori_loop(0, 16, prepare_u, 0)

    for half in range(2):
        wait_field(half, 1, d_hbm, d_mat)
        total[...] = apply_basis(u_mat, 15, c_recv[half, 15]) - d_mat[half].astype(jnp.float32)

        def predict(slot, carry):
            c_copy(half, slot).wait_recv()
            total[...] += apply_basis(u_mat, slot, c_recv[half, slot])
            return carry

        lax.fori_loop(0, 15, predict, 0)
        x_mat[half] = total[...].astype(jnp.bfloat16)
        x_rot[half] = rotated(x_mat[half])

        def adjoint(slot):
            rank = ranks_ref[0, tile, tile_at(tile, slot, -1)]
            return conj_apply(u_mat, slot, x_mat[half], x_rot[half], rank)

        def send_adjoint(slot, carry):
            a_send[half, slot] = adjoint(slot)
            a_copy(half, slot).start()
            return carry

        lax.fori_loop(0, 15, send_adjoint, 0)
        a_recv[half, 15] = adjoint(15)

    for half in range(2):
        total[...] = apply_basis(v_mat, 15, a_recv[half, 15])

        def gather(slot, carry):
            a_copy(half, slot).wait_recv()
            total[...] += apply_basis(v_mat, slot, a_recv[half, slot])
            return carry

        lax.fori_loop(0, 15, gather, 0)
        for peer in range(16):
            f_send[half, peer] = total[pl.ds(peer * 40, 40)].astype(jnp.bfloat16)

        def send_spectrum(slot, carry):
            f_copy(half, slot).start()
            return carry

        lax.fori_loop(1, 16, send_spectrum, 0)
        own = pltpu.make_async_copy(f_send.at[half, freq], f_recv.at[half, freq], out_sem.at[half])
        own.start()
        own.wait()

    for half in range(2):

        def finish_freq(slot, carry):
            f_copy(half, slot).wait()
            return carry

        lax.fori_loop(1, 16, finish_freq, 0)

        def finish_tile(slot, carry):
            c_copy(half, slot).wait_send()
            a_copy(half, slot).wait_send()
            return carry

        lax.fori_loop(0, 15, finish_tile, 0)
    out = pltpu.make_async_copy(f_recv, out_ref, out_sem.at[0])
    out.start()
    out.wait()


def traces_kernel(s_ref, onset_ref, g_ref):
    count = s_ref.shape[1]
    period = 2 * count
    scale = 1.0 / math.sqrt(count)

    def weighted(terms):
        value = None
        for factor, term in terms:
            if abs(factor) < 1e-12:
                continue
            product = term * jnp.float32(factor)
            value = product if value is None else value + product
        return jnp.zeros((8, HALF), jnp.float32) if value is None else value

    for half in range(2):
        lanes = pl.ds(half * HALF, HALF)
        for block in range(s_ref.shape[2] // 8):
            rows = pl.ds(block * 8, 8)
            onset = onset_ref[rows, lanes]
            real = [s_ref[half, f, rows, pl.ds(0, HALF)].astype(jnp.float32) for f in range(count)]
            imag = [s_ref[half, f, rows, pl.ds(HALF, HALF)].astype(jnp.float32) for f in range(count)]

            def store(time, value):
                g_ref[time, rows, lanes] = jnp.where(onset <= time, value, 0.0)

            for t in range(count // 2 + 1):
                cosine = [scale * math.cos(2 * math.pi * (((f + 1) * t) % period) / period) for f in range(count)]
                sine = [scale * math.sin(2 * math.pi * (((f + 1) * t) % period) / period) for f in range(count)]
                odd_c = weighted([(cosine[f], real[f]) for f in range(0, count, 2)])
                even_c = weighted([(cosine[f], real[f]) for f in range(1, count, 2)])
                odd_s = weighted([(sine[f], imag[f]) for f in range(0, count, 2)])
                even_s = weighted([(sine[f], imag[f]) for f in range(1, count, 2)])
                store(t, (even_c + odd_c) - (even_s + odd_s))
                if t < count - t:
                    store(count - t, (even_c - odd_c) + (even_s - odd_s))
                if 0 < t:
                    store(period - t, (even_c + odd_c) + (even_s + odd_s))
                    if count + t < period - t:
                        store(count + t, (even_c - odd_c) - (even_s - odd_s))


def body(x_field, data, u_bases, v_bases, ranks, onset):
    stations, points = x_field.shape[2:]
    tiles = 16
    count = lax.axis_size("freq")
    share = stations // count
    bf16, f32 = jnp.bfloat16, jnp.float32
    anywhere = pl.BlockSpec(memory_space=pl.ANY)
    dma = pltpu.SemaphoreType.DMA
    spectra = pl.pallas_call(
        exchange_kernel,
        name="exchange",
        out_shape=jax.ShapeDtypeStruct((2, count, share, 2 * HALF), bf16),
        in_specs=[pl.BlockSpec(memory_space=pltpu.SMEM)] + [anywhere] * 4,
        out_specs=anywhere,
        scratch_shapes=[
            pltpu.VMEM((2, stations, 2 * HALF), bf16),
            pltpu.VMEM((2, stations, 2 * HALF), bf16),
            pltpu.VMEM((2, stations, 2 * HALF), bf16),
            pltpu.VMEM((tiles, RMAX, 2, stations), bf16),
            pltpu.VMEM((tiles, RMAX, 2, stations), bf16),
            pltpu.VMEM((tiles, 2 * RMAX, stations), bf16),
            pltpu.VMEM((tiles, 2 * RMAX, stations), bf16),
            pltpu.VMEM((stations, 2 * HALF), f32),
            pltpu.VMEM((2, tiles, RMAX, 2 * HALF), bf16),
            pltpu.VMEM((2, tiles, RMAX, 2 * HALF), bf16),
            pltpu.VMEM((2, tiles, RMAX, 2 * HALF), bf16),
            pltpu.VMEM((2, tiles, RMAX, 2 * HALF), bf16),
            pltpu.VMEM((2, count, share, 2 * HALF), bf16),
            pltpu.VMEM((2, count, share, 2 * HALF), bf16),
            dma((2, 2, 2)),
            dma((tiles,)),
            dma((tiles,)),
            dma((2, 2, tiles)),
            dma((2, 2, tiles)),
            dma((2, 2, count)),
            dma((2,)),
        ],
        compiler_params=pltpu.CompilerParams(
            collective_id=0, has_side_effects=True, vmem_limit_bytes=56 << 20
        ),
    )(ranks, x_field, data, u_bases, v_bases)
    return pl.pallas_call(
        traces_kernel,
        name="traces",
        out_shape=jax.ShapeDtypeStruct((2 * count, share, points), f32),
        in_specs=[pl.BlockSpec(memory_space=pltpu.VMEM)] * 2,
        out_specs=pl.BlockSpec(memory_space=pltpu.VMEM),
        compiler_params=pltpu.CompilerParams(vmem_limit_bytes=32 << 20),
    )(spectra, onset)


def solution(mesh):
    in_specs = (
        P("freq", None, "tile", None),
        P("freq", None, "tile", None),
        P("freq", "tile", None, None, None, None),
        P("freq", None, "tile", None, None, None),
        P("freq", None, None),
        P(("tile", "freq"), None),
    )
    out_specs = P(None, ("tile", "freq"), None)
    return jax.shard_map(body, mesh=mesh, in_specs=in_specs, out_specs=out_specs, check_vma=False)
```

```python
import math

import jax
import jax.numpy as jnp
from jax import lax
from jax.experimental import pallas as pl
from jax.experimental.pallas import tpu as pltpu
from jax.sharding import PartitionSpec as P

RMAX = 96
HALF = 128
TILES = 16
LAST = TILES - 1
FREQS = 16
MESH = pl.DeviceIdType.MESH
CONTRACT_ROWS = (((0,), (0,)), ((), ()))
FREQ_ORDER = (10, 6, 9, 11, 14, 2, 8, 5, 7, 13, 15, 1, 3, 4, 12)


def weighted(terms):
    value = None
    for factor, term in terms:
        if abs(factor) < 1e-12:
            continue
        product = term * jnp.float32(factor)
        value = product if value is None else value + product
    return value


def traces(real, imag, store):
    count = len(real)
    period = 2 * count
    scale = 1.0 / math.sqrt(count)
    for t in range(count // 2 + 1):
        angles = [2 * math.pi * (((f + 1) * t) % period) / period for f in range(count)]
        cosine = [scale * math.cos(a) for a in angles]
        sine = [scale * math.sin(a) for a in angles]
        sums = []
        for factors, values in ((cosine, real), (sine, imag)):
            for start in (0, 1):
                part = weighted([(factors[f], values[f]) for f in range(start, count, 2)])
                sums.append(jnp.zeros_like(real[0]) if part is None else part)
        odd_c, even_c, odd_s, even_s = sums
        sum_c, difference_c, sum_s, difference_s = even_c + odd_c, even_c - odd_c, even_s + odd_s, even_s - odd_s
        store(t, sum_c - sum_s)
        if t < count - t:
            store(count - t, difference_c + difference_s)
        if 0 < t:
            store(period - t, sum_c + sum_s)
            if count + t < period - t:
                store(count + t, difference_c - difference_s)


def half_traces(received, onset_ref, target, half, block):
    rows = pl.ds(pl.multiple_of(block * 8, 8), 8)
    onset = onset_ref[rows, pl.ds(half * HALF, HALF)]
    count = received.shape[0]
    real = [received[f, rows, pl.ds(0, HALF)].astype(jnp.float32) for f in range(count)]
    imag = [received[f, rows, pl.ds(HALF, HALF)].astype(jnp.float32) for f in range(count)]

    def store(time, value):
        target[time, rows, :] = jnp.where(onset <= time, value, 0.0)

    traces(real, imag, store)


def exchange_kernel(
    ranks_ref, onset_ref, x_hbm, d_hbm, u_hbm, v_hbm, f_recv, first_ref,
    x_mat, x_rot, d_mat, v_raw, u_raw, v_re, v_im, u_re, u_im, total,
    c_send, c_recv, a_send, a_recv, f_send, f_first,
    load_sem, v_sem, u_sem, c_sems, a_sems, f_sems,
):
    freq = lax.axis_index("freq")
    tile = lax.axis_index("tile")
    chip, core = lax.div(tile, 2), lax.rem(tile, 2)
    freq_y, freq_x = lax.div(freq, 4), lax.rem(freq, 4)

    def tile_at(group, index, sign):
        chips = 4 + group if index < 2 else 3 - group
        peer = lax.rem(chip + sign * chips + 8, 8)
        return peer * 2 + (core if index % 2 else 1 - core)

    def freq_at(offset):
        return lax.rem(freq_y + offset // 4, 4) * 4 + lax.rem(freq_x + offset % 4, 4)

    def field_copy(source, target, half, part, index):
        return pltpu.make_async_copy(
            source.at[0, part, :, pl.ds(half * HALF, HALF)],
            target.at[half, :, pl.ds(part * HALF, HALF)],
            load_sem.at[index, half, part],
        )

    def load_field(source, target, half, index):
        for part in range(2):
            field_copy(source, target, half, part, index).start()

    def wait_field(source, target, half, index):
        for part in range(2):
            field_copy(source, target, half, part, index).wait()

    def v_copy(group, index):
        slot = 4 * group + index
        return pltpu.make_async_copy(
            v_hbm.at[0, tile_at(group, index, 1), 0, pl.ds(0, RMAX)], v_raw.at[slot], v_sem.at[slot]
        )

    def u_copy(group, index):
        slot = 4 * group + index
        return pltpu.make_async_copy(
            u_hbm.at[0, 0, tile_at(group, index, -1), pl.ds(0, RMAX)], u_raw.at[slot], u_sem.at[slot]
        )

    load_field(x_hbm, x_mat, 0, 0)
    for index in range(4):
        v_copy(0, index).start()

    barrier = pltpu.get_barrier_semaphore()
    for slot in range(LAST):
        pl.semaphore_signal(
            barrier, inc=1, device_id=(freq, tile_at(slot // 4, slot % 4, 1)), device_id_type=MESH
        )
    for offset in FREQ_ORDER:
        pl.semaphore_signal(barrier, inc=1, device_id=(freq_at(offset), tile), device_id_type=MESH)

    for group in range(1, 4):
        for index in range(4):
            v_copy(group, index).start()

    rows = lax.broadcasted_iota(jnp.int32, (2 * RMAX, 2 * RMAX), 0)
    columns = lax.broadcasted_iota(jnp.int32, (2 * RMAX, 2 * RMAX), 1)
    wanted = jnp.where(rows < RMAX, 2 * rows, 2 * (rows - RMAX) + 1)
    separate = jnp.where(columns == wanted, 1.0, 0.0).astype(jnp.bfloat16)
    levels = lax.broadcasted_iota(jnp.int32, (RMAX, 2 * HALF), 0)

    def piece(slot):
        return pl.ds(pl.multiple_of(slot * RMAX, RMAX), RMAX)

    def pieces(group):
        return pl.ds(pl.multiple_of(group * 4 * RMAX, 4 * RMAX), 4 * RMAX)

    def prepare(slot, raw, real, imag):
        interleaved = raw[slot].reshape(2 * RMAX, raw.shape[-1])
        parts = jnp.dot(separate, interleaved, preferred_element_type=jnp.float32).astype(jnp.bfloat16)
        real[piece(slot)] = parts[:RMAX]
        imag[piece(slot)] = parts[RMAX:]

    def prepare_v(group):
        for index in range(4):
            v_copy(group, index).wait()
            prepare(4 * group + index, v_raw, v_re, v_im)

    def prepare_u(group):
        for index in range(4):
            u_copy(group, index).wait()
            prepare(4 * group + index, u_raw, u_re, u_im)

    def rotated(field):
        return jnp.concatenate([field[:, HALF:], -field[:, :HALF]], axis=1)

    def conj_apply(real, imag, half, group, send, ranks):
        value = jnp.dot(real[pieces(group)], x_mat[half], preferred_element_type=jnp.float32)
        value += jnp.dot(imag[pieces(group)], x_rot[half], preferred_element_type=jnp.float32)
        for index in range(4):
            part = value[index * RMAX:(index + 1) * RMAX]
            part = jnp.where(levels < ranks(index), part, 0.0)
            send[half, piece(4 * group + index)] = part.astype(jnp.bfloat16)

    def c_copy(half, group, index):
        slot = 4 * group + index
        return pltpu.make_async_remote_copy(
            src_ref=c_send.at[half, piece(slot)], dst_ref=c_recv.at[half, piece(slot)],
            send_sem=c_sems.at[0, half, slot], recv_sem=c_sems.at[1, half, slot],
            device_id=(freq, tile_at(group, index, 1)), device_id_type=MESH,
        )

    def a_copy(half, group, index):
        slot = 4 * group + index
        return pltpu.make_async_remote_copy(
            src_ref=a_send.at[half, piece(slot)], dst_ref=a_recv.at[half, piece(slot)],
            send_sem=a_sems.at[0, half, slot], recv_sem=a_sems.at[1, half, slot],
            device_id=(freq, tile_at(group, index, -1)), device_id_type=MESH,
        )

    def f_copy(half, offset):
        return pltpu.make_async_remote_copy(
            src_ref=f_send.at[half, offset], dst_ref=(f_recv if half else f_first).at[freq],
            send_sem=f_sems.at[0, half, offset], recv_sem=f_sems.at[1, half, offset],
            device_id=(freq_at(offset), tile), device_id_type=MESH,
        )

    def each_remote(action):
        def step(group, carry):
            for index in range(4):
                action(group, index)
            return carry

        lax.fori_loop(0, 3, step, 0)
        for index in range(3):
            action(3, index)

    def coefficients(half, group):
        conj_apply(v_re, v_im, half, group, c_send, lambda index: ranks_ref[0, tile_at(group, index, 1), tile])

    def adjoint(half, group):
        conj_apply(u_re, u_im, half, group, a_send, lambda index: ranks_ref[0, tile, tile_at(group, index, -1)])

    def keep_own(send, receive, half):
        receive[half, piece(LAST)] = send[half, piece(LAST)]

    wait_field(x_hbm, x_mat, 0, 0)
    x_rot[0] = rotated(x_mat[0])
    prepare_v(0)
    coefficients(0, 0)
    pl.semaphore_wait(barrier, LAST + len(FREQ_ORDER))
    for index in range(4):
        c_copy(0, 0, index).start()

    load_field(x_hbm, x_mat, 1, 0)
    for half in range(2):
        load_field(d_hbm, d_mat, half, 1)
    for group in range(4):
        for index in range(4):
            u_copy(group, index).start()

    def first_step(group, carry):
        prepare_v(group)
        coefficients(0, group)
        for index in range(4):
            c_copy(0, group, index).start()
        return carry

    lax.fori_loop(1, 3, first_step, 0)
    prepare_v(3)
    coefficients(0, 3)
    for index in range(3):
        c_copy(0, 3, index).start()
    keep_own(c_send, c_recv, 0)

    wait_field(x_hbm, x_mat, 1, 0)
    x_rot[1] = rotated(x_mat[1])

    def second_step(group, carry):
        coefficients(1, group)
        prepare_u(group)
        return carry

    lax.fori_loop(0, 4, second_step, 0)
    keep_own(c_send, c_recv, 1)

    def send_second(group, index):
        c_copy(0, group, index).wait_send()
        c_copy(1, group, index).start()

    each_remote(send_second)

    def gather(half, copy, received, real, imag):
        def add(group):
            at = pieces(group)
            weights = received[half, at]
            partner = jnp.concatenate([-weights[:, HALF:], weights[:, :HALF]], axis=1)
            value = lax.dot_general(real[at], weights, CONTRACT_ROWS, preferred_element_type=jnp.float32)
            total[...] += value + lax.dot_general(
                imag[at], partner, CONTRACT_ROWS, preferred_element_type=jnp.float32
            )

        def step(group, carry):
            for index in range(4):
                copy(half, group, index).wait_recv()
            add(group)
            return carry

        lax.fori_loop(0, 3, step, 0)
        for index in range(3):
            copy(half, 3, index).wait_recv()
        add(3)

    for half in range(2):
        wait_field(d_hbm, d_mat, half, 1)
        total[...] = -d_mat[half].astype(jnp.float32)
        gather(half, c_copy, c_recv, u_re, u_im)
        x_mat[half] = total[...].astype(jnp.bfloat16)
        x_rot[half] = rotated(x_mat[half])

        def adjoint_step(group, carry):
            adjoint(half, group)
            for index in range(4):
                (a_copy(0, group, index) if half else c_copy(1, group, index)).wait_send()
                a_copy(half, group, index).start()
            return carry

        lax.fori_loop(0, 3, adjoint_step, 0)
        adjoint(half, 3)
        for index in range(3):
            (a_copy(0, 3, index) if half else c_copy(1, 3, index)).wait_send()
            a_copy(half, 3, index).start()
        keep_own(a_send, a_recv, half)

    share = f_recv.shape[1]
    for half in range(2):
        total[...] = jnp.zeros_like(total)
        gather(half, a_copy, a_recv, v_re, v_im)

        def spectrum(peer):
            return total[pl.ds(pl.multiple_of(peer * share, 8), share)].astype(jnp.bfloat16)

        for offset in FREQ_ORDER:
            f_send[half, offset] = spectrum(freq_at(offset))
            f_copy(half, offset).start()
        (f_recv if half else f_first)[freq] = spectrum(freq)
        if half == 0:
            for offset in FREQ_ORDER:
                f_copy(0, offset).wait()

            def trace_step(block, carry):
                half_traces(f_first, onset_ref, first_ref, 0, block)
                return carry

            lax.fori_loop(0, share // 8, trace_step, 0)

    each_remote(lambda group, index: a_copy(1, group, index).wait_send())
    for offset in FREQ_ORDER:
        f_copy(1, offset).wait()


def finish_kernel(first_ref, received, onset_ref, out_ref, second, sems):
    share = second.shape[1]
    first = pltpu.make_async_copy(first_ref, out_ref.at[:, :, pl.ds(0, HALF)], sems.at[0])
    first.start()
    copies = []
    for block in range(share // 8):
        half_traces(received, onset_ref, second, 1, block)
        rows = pl.ds(block * 8, 8)
        copy = pltpu.make_async_copy(
            second.at[:, rows], out_ref.at[:, rows, pl.ds(HALF, HALF)], sems.at[1 + block]
        )
        copy.start()
        copies.append(copy)
    first.wait()
    for copy in copies:
        copy.wait()


def body(x_field, data, u_bases, v_bases, ranks, onset):
    stations, points = x_field.shape[2:]
    share = stations // FREQS
    times = 2 * FREQS
    bf16, f32 = jnp.bfloat16, jnp.float32
    anywhere = pl.BlockSpec(memory_space=pl.ANY)
    vmem = pl.BlockSpec(memory_space=pltpu.VMEM)
    dma = pltpu.SemaphoreType.DMA
    field = pltpu.VMEM((2, stations, 2 * HALF), bf16)
    raw = pltpu.VMEM((TILES, RMAX, 2, stations), bf16)
    basis = pltpu.VMEM((TILES * RMAX, stations), bf16)
    message = pltpu.VMEM((2, TILES * RMAX, 2 * HALF), bf16)
    received, first = pl.pallas_call(
        exchange_kernel,
        name="exchange",
        out_shape=(
            pltpu.VMEM((FREQS, share, 2 * HALF), bf16),
            pltpu.VMEM((times, share, HALF), f32),
        ),
        in_specs=[pl.BlockSpec(memory_space=pltpu.SMEM), vmem] + [anywhere] * 4,
        out_specs=(vmem, vmem),
        scratch_shapes=[
            field, field, field, raw, raw, basis, basis, basis, basis,
            pltpu.VMEM((stations, 2 * HALF), f32),
            message, message, message, message,
            pltpu.VMEM((2, FREQS, share, 2 * HALF), bf16),
            pltpu.VMEM((FREQS, share, 2 * HALF), bf16),
            dma((2, 2, 2)),
            dma((TILES,)),
            dma((TILES,)),
            dma((2, 2, TILES)),
            dma((2, 2, TILES)),
            dma((2, 2, FREQS)),
        ],
        compiler_params=pltpu.CompilerParams(
            collective_id=0, has_side_effects=True, vmem_limit_bytes=56 << 20
        ),
    )(ranks, onset, x_field, data, u_bases, v_bases)
    return pl.pallas_call(
        finish_kernel,
        name="finish",
        out_shape=jax.ShapeDtypeStruct((times, share, points), f32),
        in_specs=[vmem] * 3,
        out_specs=anywhere,
        scratch_shapes=[pltpu.VMEM((times, share, HALF), f32), dma((1 + share // 8,))],
        compiler_params=pltpu.CompilerParams(vmem_limit_bytes=32 << 20),
    )(first, received, onset)


def solution(mesh):
    in_specs = (
        P("freq", None, "tile", None),
        P("freq", None, "tile", None),
        P("freq", "tile", None, None, None, None),
        P("freq", None, "tile", None, None, None),
        P("freq", None, None),
        P(("tile", "freq"), None),
    )
    out_specs = P(None, ("tile", "freq"), None)
    return jax.shard_map(body, mesh=mesh, in_specs=in_specs, out_specs=out_specs, check_vma=False)
```

```python
import math

import jax
import jax.numpy as jnp
from jax import lax
from jax.experimental import pallas as pl
from jax.experimental.pallas import tpu as pltpu
from jax.sharding import PartitionSpec as P

RMAX = 96
HALF = 128
TILES = 16
LAST = TILES - 1
FREQS = 16
MESH = pl.DeviceIdType.MESH
CONTRACT_ROWS = (((0,), (0,)), ((), ()))
FREQ_ORDER = (10, 6, 9, 11, 14, 2, 8, 5, 7, 13, 15, 1, 3, 4, 12)


def weighted(terms):
    value = None
    for factor, term in terms:
        if abs(factor) < 1e-12:
            continue
        product = term * jnp.float32(factor)
        value = product if value is None else value + product
    return value


def traces(real, imag, store):
    count = len(real)
    period = 2 * count
    scale = 1.0 / math.sqrt(count)
    for t in range(count // 2 + 1):
        angles = [2 * math.pi * (((f + 1) * t) % period) / period for f in range(count)]
        cosine = [scale * math.cos(a) for a in angles]
        sine = [scale * math.sin(a) for a in angles]
        sums = []
        for factors, values in ((cosine, real), (sine, imag)):
            for start in (0, 1):
                part = weighted([(factors[f], values[f]) for f in range(start, count, 2)])
                sums.append(jnp.zeros_like(real[0]) if part is None else part)
        odd_c, even_c, odd_s, even_s = sums
        sum_c, difference_c, sum_s, difference_s = even_c + odd_c, even_c - odd_c, even_s + odd_s, even_s - odd_s
        store(t, sum_c - sum_s)
        if t < count - t:
            store(count - t, difference_c + difference_s)
        if 0 < t:
            store(period - t, sum_c + sum_s)
            if count + t < period - t:
                store(count + t, difference_c - difference_s)


def half_traces(received, onset_ref, target, half, block):
    rows = pl.ds(pl.multiple_of(block * 8, 8), 8)
    onset = onset_ref[rows, pl.ds(half * HALF, HALF)]
    count = received.shape[0]
    real = [received[f, rows, pl.ds(0, HALF)].astype(jnp.float32) for f in range(count)]
    imag = [received[f, rows, pl.ds(HALF, HALF)].astype(jnp.float32) for f in range(count)]

    def store(time, value):
        target[time, rows, :] = jnp.where(onset <= time, value, 0.0)

    traces(real, imag, store)


def exchange_kernel(
    ranks_ref, onset_ref, x_hbm, d_hbm, u_hbm, v_hbm, f_recv, first_ref,
    x_mat, x_rot, d_mat, v_raw, u_raw, v_re, v_im, u_re, u_im, total,
    c_send, c_recv, a_send, a_recv, f_send, f_first,
    load_sem, v_sem, u_sem, c_sems, a_sems, f_sems,
):
    freq = lax.axis_index("freq")
    tile = lax.axis_index("tile")
    chip, core = lax.div(tile, 2), lax.rem(tile, 2)
    freq_y, freq_x = lax.div(freq, 4), lax.rem(freq, 4)

    def tile_at(group, index, sign):
        chips = 7 - group if index < 2 else lax.rem(group + 1, 4)
        peer = lax.rem(chip + sign * chips + 8, 8)
        return peer * 2 + (core if index % 2 else 1 - core)

    def freq_at(offset):
        return lax.rem(freq_y + offset // 4, 4) * 4 + lax.rem(freq_x + offset % 4, 4)

    def field_copy(source, target, half, part, index):
        return pltpu.make_async_copy(
            source.at[0, part, :, pl.ds(half * HALF, HALF)],
            target.at[half, :, pl.ds(part * HALF, HALF)],
            load_sem.at[index, half, part],
        )

    def load_field(source, target, half, index):
        for part in range(2):
            field_copy(source, target, half, part, index).start()

    def wait_field(source, target, half, index):
        for part in range(2):
            field_copy(source, target, half, part, index).wait()

    def v_copy(group, index):
        slot = 4 * group + index
        return pltpu.make_async_copy(
            v_hbm.at[0, tile_at(group, index, 1), 0, pl.ds(0, RMAX)], v_raw.at[slot], v_sem.at[slot]
        )

    def u_copy(group, index):
        slot = 4 * group + index
        return pltpu.make_async_copy(
            u_hbm.at[0, 0, tile_at(group, index, -1), pl.ds(0, RMAX)], u_raw.at[slot], u_sem.at[slot]
        )

    load_field(x_hbm, x_mat, 0, 0)
    for index in range(4):
        v_copy(0, index).start()

    barrier = pltpu.get_barrier_semaphore()
    for slot in range(LAST):
        pl.semaphore_signal(
            barrier, inc=1, device_id=(freq, tile_at(slot // 4, slot % 4, 1)), device_id_type=MESH
        )
    for offset in FREQ_ORDER:
        pl.semaphore_signal(barrier, inc=1, device_id=(freq_at(offset), tile), device_id_type=MESH)

    for group in range(1, 4):
        for index in range(4):
            v_copy(group, index).start()

    rows = lax.broadcasted_iota(jnp.int32, (2 * RMAX, 2 * RMAX), 0)
    columns = lax.broadcasted_iota(jnp.int32, (2 * RMAX, 2 * RMAX), 1)
    wanted = jnp.where(rows < RMAX, 2 * rows, 2 * (rows - RMAX) + 1)
    separate = jnp.where(columns == wanted, 1.0, 0.0).astype(jnp.bfloat16)
    levels = lax.broadcasted_iota(jnp.int32, (RMAX, 2 * HALF), 0)

    def piece(slot):
        return pl.ds(pl.multiple_of(slot * RMAX, RMAX), RMAX)

    def pieces(group):
        return pl.ds(pl.multiple_of(group * 4 * RMAX, 4 * RMAX), 4 * RMAX)

    def prepare(slot, raw, real, imag):
        interleaved = raw[slot].reshape(2 * RMAX, raw.shape[-1])
        parts = jnp.dot(separate, interleaved, preferred_element_type=jnp.float32).astype(jnp.bfloat16)
        real[piece(slot)] = parts[:RMAX]
        imag[piece(slot)] = parts[RMAX:]

    def prepare_v(group):
        for index in range(4):
            v_copy(group, index).wait()
            prepare(4 * group + index, v_raw, v_re, v_im)

    def prepare_u(group):
        for index in range(4):
            u_copy(group, index).wait()
            prepare(4 * group + index, u_raw, u_re, u_im)

    def rotated(field):
        return jnp.concatenate([field[:, HALF:], -field[:, :HALF]], axis=1)

    def conj_apply(real, imag, half, group, send, ranks):
        value = jnp.dot(real[pieces(group)], x_mat[half], preferred_element_type=jnp.float32)
        value += jnp.dot(imag[pieces(group)], x_rot[half], preferred_element_type=jnp.float32)
        for index in range(4):
            part = value[index * RMAX:(index + 1) * RMAX]
            part = jnp.where(levels < ranks(index), part, 0.0)
            send[half, piece(4 * group + index)] = part.astype(jnp.bfloat16)

    def c_copy(half, group, index):
        slot = 4 * group + index
        return pltpu.make_async_remote_copy(
            src_ref=c_send.at[half, piece(slot)], dst_ref=c_recv.at[half, piece(slot)],
            send_sem=c_sems.at[0, half, slot], recv_sem=c_sems.at[1, half, slot],
            device_id=(freq, tile_at(group, index, 1)), device_id_type=MESH,
        )

    def a_copy(half, group, index):
        slot = 4 * group + index
        return pltpu.make_async_remote_copy(
            src_ref=a_send.at[half, piece(slot)], dst_ref=a_recv.at[half, piece(slot)],
            send_sem=a_sems.at[0, half, slot], recv_sem=a_sems.at[1, half, slot],
            device_id=(freq, tile_at(group, index, -1)), device_id_type=MESH,
        )

    def f_copy(half, offset):
        return pltpu.make_async_remote_copy(
            src_ref=f_send.at[half, offset], dst_ref=(f_recv if half else f_first).at[freq],
            send_sem=f_sems.at[0, half, offset], recv_sem=f_sems.at[1, half, offset],
            device_id=(freq_at(offset), tile), device_id_type=MESH,
        )

    def each_remote(action):
        def step(group, carry):
            for index in range(4):
                action(group, index)
            return carry

        lax.fori_loop(0, 3, step, 0)
        for index in range(3):
            action(3, index)

    def coefficients(half, group):
        conj_apply(v_re, v_im, half, group, c_send, lambda index: ranks_ref[0, tile_at(group, index, 1), tile])

    def adjoint(half, group):
        conj_apply(u_re, u_im, half, group, a_send, lambda index: ranks_ref[0, tile, tile_at(group, index, -1)])

    def keep_own(send, receive, half):
        receive[half, piece(LAST)] = send[half, piece(LAST)]

    wait_field(x_hbm, x_mat, 0, 0)
    x_rot[0] = rotated(x_mat[0])
    prepare_v(0)
    coefficients(0, 0)
    pl.semaphore_wait(barrier, LAST + len(FREQ_ORDER))
    for index in range(4):
        c_copy(0, 0, index).start()

    load_field(x_hbm, x_mat, 1, 0)
    for half in range(2):
        load_field(d_hbm, d_mat, half, 1)
    for group in range(4):
        for index in range(4):
            u_copy(group, index).start()

    def first_step(group, carry):
        prepare_v(group)
        coefficients(0, group)
        for index in range(4):
            c_copy(0, group, index).start()
        return carry

    lax.fori_loop(1, 3, first_step, 0)
    prepare_v(3)
    coefficients(0, 3)
    for index in range(3):
        c_copy(0, 3, index).start()
    keep_own(c_send, c_recv, 0)

    wait_field(x_hbm, x_mat, 1, 0)
    x_rot[1] = rotated(x_mat[1])

    def second_step(group, carry):
        coefficients(1, group)
        prepare_u(group)
        return carry

    lax.fori_loop(0, 4, second_step, 0)
    keep_own(c_send, c_recv, 1)

    def send_second(group, index):
        c_copy(1, group, index).start()

    each_remote(send_second)

    def gather(half, copy, received, real, imag):
        def add(group):
            at = pieces(group)
            weights = received[half, at]
            partner = jnp.concatenate([-weights[:, HALF:], weights[:, :HALF]], axis=1)
            value = lax.dot_general(real[at], weights, CONTRACT_ROWS, preferred_element_type=jnp.float32)
            total[...] += value + lax.dot_general(
                imag[at], partner, CONTRACT_ROWS, preferred_element_type=jnp.float32
            )

        def step(group, carry):
            for index in range(4):
                copy(half, group, index).wait_recv()
            add(group)
            return carry

        lax.fori_loop(0, 3, step, 0)
        for index in range(3):
            copy(half, 3, index).wait_recv()
        add(3)

    for half in range(2):
        wait_field(d_hbm, d_mat, half, 1)
        total[...] = -d_mat[half].astype(jnp.float32)
        gather(half, c_copy, c_recv, u_re, u_im)
        x_mat[half] = total[...].astype(jnp.bfloat16)
        x_rot[half] = rotated(x_mat[half])

        def adjoint_step(group, carry):
            adjoint(half, group)
            for index in range(4):
                a_copy(half, group, index).start()
            return carry

        lax.fori_loop(0, 3, adjoint_step, 0)
        adjoint(half, 3)
        for index in range(3):
            a_copy(half, 3, index).start()
        keep_own(a_send, a_recv, half)

    share = f_recv.shape[1]
    for half in range(2):
        total[...] = jnp.zeros_like(total)
        gather(half, a_copy, a_recv, v_re, v_im)

        def spectrum(peer):
            return total[pl.ds(pl.multiple_of(peer * share, 8), share)].astype(jnp.bfloat16)

        for offset in FREQ_ORDER:
            f_send[half, offset] = spectrum(freq_at(offset))
            f_copy(half, offset).start()
        (f_recv if half else f_first)[freq] = spectrum(freq)
        if half == 0:
            for offset in FREQ_ORDER:
                f_copy(0, offset).wait()

            def trace_step(block, carry):
                half_traces(f_first, onset_ref, first_ref, 0, block)
                return carry

            lax.fori_loop(0, share // 8, trace_step, 0)

    for copy in (c_copy, a_copy):
        for half in range(2):
            each_remote(lambda group, index: copy(half, group, index).wait_send())
    for offset in FREQ_ORDER:
        f_copy(1, offset).wait()


def finish_kernel(first_ref, received, onset_ref, out_ref, second, sems):
    share = second.shape[1]
    first = pltpu.make_async_copy(first_ref, out_ref.at[:, :, pl.ds(0, HALF)], sems.at[0])
    first.start()
    copies = []
    for block in range(share // 8):
        half_traces(received, onset_ref, second, 1, block)
        rows = pl.ds(block * 8, 8)
        copy = pltpu.make_async_copy(
            second.at[:, rows], out_ref.at[:, rows, pl.ds(HALF, HALF)], sems.at[1 + block]
        )
        copy.start()
        copies.append(copy)
    first.wait()
    for copy in copies:
        copy.wait()


def body(x_field, data, u_bases, v_bases, ranks, onset):
    stations, points = x_field.shape[2:]
    share = stations // FREQS
    times = 2 * FREQS
    bf16, f32 = jnp.bfloat16, jnp.float32
    anywhere = pl.BlockSpec(memory_space=pl.ANY)
    vmem = pl.BlockSpec(memory_space=pltpu.VMEM)
    dma = pltpu.SemaphoreType.DMA
    field = pltpu.VMEM((2, stations, 2 * HALF), bf16)
    raw = pltpu.VMEM((TILES, RMAX, 2, stations), bf16)
    basis = pltpu.VMEM((TILES * RMAX, stations), bf16)
    message = pltpu.VMEM((2, TILES * RMAX, 2 * HALF), bf16)
    received, first = pl.pallas_call(
        exchange_kernel,
        name="exchange",
        out_shape=(
            pltpu.VMEM((FREQS, share, 2 * HALF), bf16),
            pltpu.VMEM((times, share, HALF), f32),
        ),
        in_specs=[pl.BlockSpec(memory_space=pltpu.SMEM), vmem] + [anywhere] * 4,
        out_specs=(vmem, vmem),
        scratch_shapes=[
            field, field, field, raw, raw, basis, basis, basis, basis,
            pltpu.VMEM((stations, 2 * HALF), f32),
            message, message, message, message,
            pltpu.VMEM((2, FREQS, share, 2 * HALF), bf16),
            pltpu.VMEM((FREQS, share, 2 * HALF), bf16),
            dma((2, 2, 2)),
            dma((TILES,)),
            dma((TILES,)),
            dma((2, 2, TILES)),
            dma((2, 2, TILES)),
            dma((2, 2, FREQS)),
        ],
        compiler_params=pltpu.CompilerParams(
            collective_id=0, has_side_effects=True, vmem_limit_bytes=56 << 20
        ),
    )(ranks, onset, x_field, data, u_bases, v_bases)
    return pl.pallas_call(
        finish_kernel,
        name="finish",
        out_shape=jax.ShapeDtypeStruct((times, share, points), f32),
        in_specs=[vmem] * 3,
        out_specs=anywhere,
        scratch_shapes=[pltpu.VMEM((times, share, HALF), f32), dma((1 + share // 8,))],
        compiler_params=pltpu.CompilerParams(vmem_limit_bytes=32 << 20),
    )(first, received, onset)


def solution(mesh):
    in_specs = (
        P("freq", None, "tile", None),
        P("freq", None, "tile", None),
        P("freq", "tile", None, None, None, None),
        P("freq", None, "tile", None, None, None),
        P("freq", None, None),
        P(("tile", "freq"), None),
    )
    out_specs = P(None, ("tile", "freq"), None)
    return jax.shard_map(body, mesh=mesh, in_specs=in_specs, out_specs=out_specs, check_vma=False)
```

```python
import math

import jax
import jax.numpy as jnp
from jax import lax
from jax.experimental import pallas as pl
from jax.experimental.pallas import tpu as pltpu
from jax.sharding import PartitionSpec as P

RMAX = 96
HALF = 128
TILES = 16
LAST = TILES - 1
FREQS = 16
MESH = pl.DeviceIdType.MESH
CONTRACT_ROWS = (((0,), (0,)), ((), ()))
FREQ_ORDER = (10, 6, 9, 11, 14, 2, 8, 5, 7, 13, 15, 1, 3, 4, 12)


def weighted(terms):
    value = None
    for factor, term in terms:
        if abs(factor) < 1e-12:
            continue
        product = term * jnp.float32(factor)
        value = product if value is None else value + product
    return value


def traces(real, imag, store):
    count = len(real)
    period = 2 * count
    scale = 1.0 / math.sqrt(count)
    for t in range(count // 2 + 1):
        angles = [2 * math.pi * (((f + 1) * t) % period) / period for f in range(count)]
        cosine = [scale * math.cos(a) for a in angles]
        sine = [scale * math.sin(a) for a in angles]
        sums = []
        for factors, values in ((cosine, real), (sine, imag)):
            for start in (0, 1):
                part = weighted([(factors[f], values[f]) for f in range(start, count, 2)])
                sums.append(jnp.zeros_like(real[0]) if part is None else part)
        odd_c, even_c, odd_s, even_s = sums
        sum_c, difference_c, sum_s, difference_s = even_c + odd_c, even_c - odd_c, even_s + odd_s, even_s - odd_s
        store(t, sum_c - sum_s)
        if t < count - t:
            store(count - t, difference_c + difference_s)
        if 0 < t:
            store(period - t, sum_c + sum_s)
            if count + t < period - t:
                store(count + t, difference_c - difference_s)


def half_traces(received, onset_ref, target, half, block):
    rows = pl.ds(pl.multiple_of(block * 8, 8), 8)
    onset = onset_ref[rows, pl.ds(half * HALF, HALF)]
    count = received.shape[0]
    real = [received[f, rows, pl.ds(0, HALF)].astype(jnp.float32) for f in range(count)]
    imag = [received[f, rows, pl.ds(HALF, HALF)].astype(jnp.float32) for f in range(count)]

    def store(time, value):
        target[time, rows, :] = jnp.where(onset <= time, value, 0.0)

    traces(real, imag, store)


def exchange_kernel(
    ranks_ref, onset_ref, x_hbm, d_hbm, u_hbm, v_hbm, f_recv, first_ref,
    x_mat, x_rot, d_mat, v_raw, u_raw, v_re, v_im, u_re, u_im, total,
    c_send, c_recv, a_send, a_recv, f_send, f_first,
    load_sem, v_sem, u_sem, c_sems, a_sems, f_sems,
):
    freq = lax.axis_index("freq")
    tile = lax.axis_index("tile")
    chip, core = lax.div(tile, 2), lax.rem(tile, 2)
    freq_y, freq_x = lax.div(freq, 4), lax.rem(freq, 4)

    def tile_at(group, index, sign):
        chips = 7 - group if index < 2 else lax.rem(group + 1, 4)
        peer = lax.rem(chip + sign * chips + 8, 8)
        return peer * 2 + (core if index % 2 else 1 - core)

    def freq_at(offset):
        return lax.rem(freq_y + offset // 4, 4) * 4 + lax.rem(freq_x + offset % 4, 4)

    def field_copy(source, target, half, part, index):
        return pltpu.make_async_copy(
            source.at[0, part, :, pl.ds(half * HALF, HALF)],
            target.at[half, :, pl.ds(part * HALF, HALF)],
            load_sem.at[index, half, part],
        )

    def load_field(source, target, half, index):
        for part in range(2):
            field_copy(source, target, half, part, index).start()

    def wait_field(source, target, half, index):
        for part in range(2):
            field_copy(source, target, half, part, index).wait()

    def v_copy(group, index):
        slot = 4 * group + index
        return pltpu.make_async_copy(
            v_hbm.at[0, tile_at(group, index, 1), 0, pl.ds(0, RMAX)], v_raw.at[slot], v_sem.at[slot]
        )

    def u_copy(group, index):
        slot = 4 * group + index
        return pltpu.make_async_copy(
            u_hbm.at[0, 0, tile_at(group, index, -1), pl.ds(0, RMAX)], u_raw.at[slot], u_sem.at[slot]
        )

    load_field(x_hbm, x_mat, 0, 0)
    for index in range(4):
        v_copy(0, index).start()

    barrier = pltpu.get_barrier_semaphore()
    for slot in range(LAST):
        pl.semaphore_signal(
            barrier, inc=1, device_id=(freq, tile_at(slot // 4, slot % 4, 1)), device_id_type=MESH
        )
    for offset in FREQ_ORDER:
        pl.semaphore_signal(barrier, inc=1, device_id=(freq_at(offset), tile), device_id_type=MESH)

    for group in range(1, 4):
        for index in range(4):
            v_copy(group, index).start()

    rows = lax.broadcasted_iota(jnp.int32, (2 * RMAX, 2 * RMAX), 0)
    columns = lax.broadcasted_iota(jnp.int32, (2 * RMAX, 2 * RMAX), 1)
    wanted = jnp.where(rows < RMAX, 2 * rows, 2 * (rows - RMAX) + 1)
    separate = jnp.where(columns == wanted, 1.0, 0.0).astype(jnp.bfloat16)
    levels = lax.broadcasted_iota(jnp.int32, (RMAX, 2 * HALF), 0)

    def piece(slot):
        return pl.ds(pl.multiple_of(slot * RMAX, RMAX), RMAX)

    def pieces(group):
        return pl.ds(pl.multiple_of(group * 4 * RMAX, 4 * RMAX), 4 * RMAX)

    def prepare(slot, raw, real, imag):
        interleaved = raw[slot].reshape(2 * RMAX, raw.shape[-1])
        parts = jnp.dot(separate, interleaved, preferred_element_type=jnp.float32).astype(jnp.bfloat16)
        real[piece(slot)] = parts[:RMAX]
        imag[piece(slot)] = parts[RMAX:]

    def prepare_v(group):
        for index in range(4):
            v_copy(group, index).wait()
            prepare(4 * group + index, v_raw, v_re, v_im)

    def prepare_u(group):
        for index in range(4):
            u_copy(group, index).wait()
            prepare(4 * group + index, u_raw, u_re, u_im)

    def rotated(field):
        return jnp.concatenate([field[:, HALF:], -field[:, :HALF]], axis=1)

    def conj_apply(real, imag, half, group, send, ranks):
        value = jnp.dot(real[pieces(group)], x_mat[half], preferred_element_type=jnp.float32)
        value += jnp.dot(imag[pieces(group)], x_rot[half], preferred_element_type=jnp.float32)
        for index in range(4):
            part = value[index * RMAX:(index + 1) * RMAX]
            part = jnp.where(levels < ranks(index), part, 0.0)
            send[half, piece(4 * group + index)] = part.astype(jnp.bfloat16)

    def c_copy(half, group, index):
        slot = 4 * group + index
        return pltpu.make_async_remote_copy(
            src_ref=c_send.at[half, piece(slot)], dst_ref=c_recv.at[half, piece(slot)],
            send_sem=c_sems.at[0, half, slot], recv_sem=c_sems.at[1, half, slot],
            device_id=(freq, tile_at(group, index, 1)), device_id_type=MESH,
        )

    def a_copy(half, group, index):
        slot = 4 * group + index
        return pltpu.make_async_remote_copy(
            src_ref=a_send.at[half, piece(slot)], dst_ref=a_recv.at[half, piece(slot)],
            send_sem=a_sems.at[0, half, slot], recv_sem=a_sems.at[1, half, slot],
            device_id=(freq, tile_at(group, index, -1)), device_id_type=MESH,
        )

    def f_copy(half, offset):
        return pltpu.make_async_remote_copy(
            src_ref=f_send.at[half, offset], dst_ref=(f_recv if half else f_first).at[freq],
            send_sem=f_sems.at[0, half, offset], recv_sem=f_sems.at[1, half, offset],
            device_id=(freq_at(offset), tile), device_id_type=MESH,
        )

    def each_remote(action):
        def step(group, carry):
            for index in range(4):
                action(group, index)
            return carry

        lax.fori_loop(0, 3, step, 0)
        for index in range(3):
            action(3, index)

    def coefficients(half, group):
        conj_apply(v_re, v_im, half, group, c_send, lambda index: ranks_ref[0, tile_at(group, index, 1), tile])

    def adjoint(half, group):
        conj_apply(u_re, u_im, half, group, a_send, lambda index: ranks_ref[0, tile, tile_at(group, index, -1)])

    def keep_own(send, receive, half):
        receive[half, piece(LAST)] = send[half, piece(LAST)]

    wait_field(x_hbm, x_mat, 0, 0)
    x_rot[0] = rotated(x_mat[0])
    prepare_v(0)
    coefficients(0, 0)
    pl.semaphore_wait(barrier, LAST + len(FREQ_ORDER))
    for index in range(4):
        c_copy(0, 0, index).start()

    load_field(x_hbm, x_mat, 1, 0)
    for half in range(2):
        load_field(d_hbm, d_mat, half, 1)
    for group in range(4):
        for index in range(4):
            u_copy(group, index).start()

    def first_step(group, carry):
        prepare_v(group)
        coefficients(0, group)
        for index in range(4):
            c_copy(0, group, index).start()
        return carry

    lax.fori_loop(1, 3, first_step, 0)
    prepare_v(3)
    coefficients(0, 3)
    for index in range(3):
        c_copy(0, 3, index).start()
    keep_own(c_send, c_recv, 0)

    wait_field(x_hbm, x_mat, 1, 0)
    x_rot[1] = rotated(x_mat[1])

    def second_step(group, carry):
        coefficients(1, group)
        prepare_u(group)
        return carry

    lax.fori_loop(0, 4, second_step, 0)
    keep_own(c_send, c_recv, 1)

    def send_second(group, index):
        c_copy(1, group, index).start()

    each_remote(send_second)

    def gather(half, copy, received, real, imag, split=False):
        def add(slot, count=4):
            at = pl.ds(pl.multiple_of(slot * RMAX, 2 * RMAX), count * RMAX)
            weights = received[half, at]
            partner = jnp.concatenate([-weights[:, HALF:], weights[:, :HALF]], axis=1)
            value = lax.dot_general(real[at], weights, CONTRACT_ROWS, preferred_element_type=jnp.float32)
            total[...] += value + lax.dot_general(
                imag[at], partner, CONTRACT_ROWS, preferred_element_type=jnp.float32
            )

        def step(group, carry):
            for index in range(4):
                copy(half, group, index).wait_recv()
            add(4 * group)
            return carry

        if split:
            copy(half, 3, 2).wait_recv()
            add(14, 2)
        lax.fori_loop(0, 3, step, 0)
        for index in range(2 if split else 3):
            copy(half, 3, index).wait_recv()
        add(12, 2 if split else 4)

    for half in range(2):
        wait_field(d_hbm, d_mat, half, 1)
        total[...] = -d_mat[half].astype(jnp.float32)
        gather(half, c_copy, c_recv, u_re, u_im)
        x_mat[half] = total[...].astype(jnp.bfloat16)
        x_rot[half] = rotated(x_mat[half])

        def adjoint_step(group, carry):
            adjoint(half, group)
            for index in range(4):
                a_copy(half, group, index).start()
            return carry

        lax.fori_loop(0, 3, adjoint_step, 0)
        adjoint(half, 3)
        for index in range(3):
            a_copy(half, 3, index).start()
        keep_own(a_send, a_recv, half)

    share = f_recv.shape[1]
    for half in range(2):
        total[...] = jnp.zeros_like(total)
        gather(half, a_copy, a_recv, v_re, v_im, half == 1)

        def spectrum(peer):
            return total[pl.ds(pl.multiple_of(peer * share, 8), share)].astype(jnp.bfloat16)

        for offset in FREQ_ORDER:
            f_send[half, offset] = spectrum(freq_at(offset))
            f_copy(half, offset).start()
        (f_recv if half else f_first)[freq] = spectrum(freq)
        if half == 0:
            for offset in FREQ_ORDER:
                f_copy(0, offset).wait()

            def trace_step(block, carry):
                half_traces(f_first, onset_ref, first_ref, 0, block)
                return carry

            lax.fori_loop(0, share // 8, trace_step, 0)

    for copy in (c_copy, a_copy):
        for half in range(2):
            each_remote(lambda group, index: copy(half, group, index).wait_send())
    for offset in FREQ_ORDER:
        f_copy(1, offset).wait()


def finish_kernel(first_ref, received, onset_ref, out_ref, second, sems):
    share = second.shape[1]
    first = pltpu.make_async_copy(first_ref, out_ref.at[:, :, pl.ds(0, HALF)], sems.at[0])
    first.start()
    copies = []
    for block in range(share // 8):
        half_traces(received, onset_ref, second, 1, block)
        rows = pl.ds(block * 8, 8)
        copy = pltpu.make_async_copy(
            second.at[:, rows], out_ref.at[:, rows, pl.ds(HALF, HALF)], sems.at[1 + block]
        )
        copy.start()
        copies.append(copy)
    first.wait()
    for copy in copies:
        copy.wait()


def body(x_field, data, u_bases, v_bases, ranks, onset):
    stations, points = x_field.shape[2:]
    share = stations // FREQS
    times = 2 * FREQS
    bf16, f32 = jnp.bfloat16, jnp.float32
    anywhere = pl.BlockSpec(memory_space=pl.ANY)
    vmem = pl.BlockSpec(memory_space=pltpu.VMEM)
    dma = pltpu.SemaphoreType.DMA
    field = pltpu.VMEM((2, stations, 2 * HALF), bf16)
    raw = pltpu.VMEM((TILES, RMAX, 2, stations), bf16)
    basis = pltpu.VMEM((TILES * RMAX, stations), bf16)
    message = pltpu.VMEM((2, TILES * RMAX, 2 * HALF), bf16)
    received, first = pl.pallas_call(
        exchange_kernel,
        name="exchange",
        out_shape=(
            pltpu.VMEM((FREQS, share, 2 * HALF), bf16),
            pltpu.VMEM((times, share, HALF), f32),
        ),
        in_specs=[pl.BlockSpec(memory_space=pltpu.SMEM), vmem] + [anywhere] * 4,
        out_specs=(vmem, vmem),
        scratch_shapes=[
            field, field, field, raw, raw, basis, basis, basis, basis,
            pltpu.VMEM((stations, 2 * HALF), f32),
            message, message, message, message,
            pltpu.VMEM((2, FREQS, share, 2 * HALF), bf16),
            pltpu.VMEM((FREQS, share, 2 * HALF), bf16),
            dma((2, 2, 2)),
            dma((TILES,)),
            dma((TILES,)),
            dma((2, 2, TILES)),
            dma((2, 2, TILES)),
            dma((2, 2, FREQS)),
        ],
        compiler_params=pltpu.CompilerParams(
            collective_id=0, has_side_effects=True, vmem_limit_bytes=56 << 20
        ),
    )(ranks, onset, x_field, data, u_bases, v_bases)
    return pl.pallas_call(
        finish_kernel,
        name="finish",
        out_shape=jax.ShapeDtypeStruct((times, share, points), f32),
        in_specs=[vmem] * 3,
        out_specs=anywhere,
        scratch_shapes=[pltpu.VMEM((times, share, HALF), f32), dma((1 + share // 8,))],
        compiler_params=pltpu.CompilerParams(vmem_limit_bytes=32 << 20),
    )(first, received, onset)


def solution(mesh):
    in_specs = (
        P("freq", None, "tile", None),
        P("freq", None, "tile", None),
        P("freq", "tile", None, None, None, None),
        P("freq", None, "tile", None, None, None),
        P("freq", None, None),
        P(("tile", "freq"), None),
    )
    out_specs = P(None, ("tile", "freq"), None)
    return jax.shard_map(body, mesh=mesh, in_specs=in_specs, out_specs=out_specs, check_vma=False)
```
